32 devices in a mesh: dp: 8 (over z, x), fsdp: 4 (over y, core).
Axes of the slice: x: 2, y: 2, z: 4, core: 2. Of those that a mesh axis runs over, the one named last changes fastest.
Arguments:
- tokens: bfloat16 [8192, 1280], P(('dp', 'fsdp')), may hold values from -6 to 6
- teacher: bfloat16 [8192, 1280], P(('dp', 'fsdp')), may hold values from -6 to 6
- series_ids: int32 [8192], P(('dp', 'fsdp')), may hold values from 0 to 1, as said below
- live_mask: int32 [8192], P(('dp', 'fsdp')), may hold values from 0 to 1, as said below
- gain_one: bfloat16 [1280], P(('dp', 'fsdp')), may hold values from 0.25 to 1.75
- query_scale: bfloat16 [80], replicated, may hold values from 0.69921875 to 2.1875
- query_weight: bfloat16 [1280, 1280], P(('dp', 'fsdp')), may hold values from -0.15625 to 0.15625
- key_weight: bfloat16 [1280, 1280], P(('dp', 'fsdp')), may hold values from -0.15625 to 0.15625
- value_weight: bfloat16 [1280, 1280], P(('dp', 'fsdp')), may hold values from -0.15625 to 0.15625
- attn_out_weight: bfloat16 [1280, 1280], P(('dp', 'fsdp')), may hold values from -0.625 to 0.625
- gain_two: bfloat16 [1280], P(('dp', 'fsdp')), may hold values from 0.25 to 1.75
- hidden_weight: bfloat16 [1280, 1280], P(('dp', 'fsdp')), may hold values from -0.15625 to 0.15625
- hidden_bias: bfloat16 [1280], P(('dp', 'fsdp')), may hold values from -1.5 to 1.5
- output_weight: bfloat16 [1280, 1280], P(('dp', 'fsdp')), may hold values from -0.15625 to 0.15625
- output_bias: bfloat16 [1280], P(('dp', 'fsdp')), may hold values from -1.5 to 1.5
Outputs:
- block_out: bfloat16 [8192, 1280], P(('dp', 'fsdp'))
- loss_value: float32 [], replicated
- grad_tokens: float32 [8192, 1280], P(('dp', 'fsdp'))
- grad_gain_one: float32 [1280], P(('dp', 'fsdp'))
- grad_query_scale: float32 [80], replicated
- grad_query: float32 [1280, 1280], P(('dp', 'fsdp'))
- grad_key: float32 [1280, 1280], P(('dp', 'fsdp'))
- grad_value: float32 [1280, 1280], P(('dp', 'fsdp'))
- grad_attn_out: float32 [1280, 1280], P(('dp', 'fsdp'))
- grad_gain_two: float32 [1280], P(('dp', 'fsdp'))
- grad_hidden: float32 [1280, 1280], P(('dp', 'fsdp'))
- grad_hidden_bias: float32 [1280], P(('dp', 'fsdp'))
- grad_output: float32 [1280, 1280], P(('dp', 'fsdp'))
- grad_output_bias: float32 [1280], P(('dp', 'fsdp'))
The draws below stay inside these ranges and needn't reach their ends.
Inputs may be any that keep to these rules, and one draw needn't show every extreme that they name: `series_ids`: each aligned block of 1024 slots holds two series: series 0 on its first slots, series 1 on the rest, each of at least 341 slots. `live_mask`: the live slots of a series are its first ones; at least a quarter of each series, rounded down, is live.
All inputs are finite; a program needn't handle non-finite values.
Results may differ from the reference program's by a relative error of at most 0.012.
The reference program's roundings to bfloat16 on the way count: a program that leaves them out, or rounds other values in their place, can miss the bound.
Values may be sent and summed in bfloat16 or wider, within the bound.
No kernel may reach another device: no remote copies, remote signals or barrier semaphores. Data moves between devices by JAX's collectives and lax.ppermute only.
A program may use at most 192 MiB of HBM per device.

```python
import math
import jax
import jax.numpy as jnp
from jax import lax

D = 1280
HEADS = 16
HEAD_DIM = 80
FF = 1280
GROUP = 1024
LEAST = 341
TOKENS = 8192


def series_layout(key):
    groups = TOKENS // GROUP
    split = jax.random.randint(jax.random.fold_in(key, 101), (groups, 1), LEAST, GROUP - LEAST + 1, dtype=jnp.int32)
    slot = jnp.arange(GROUP, dtype=jnp.int32)[None, :]
    series = (slot >= split).astype(jnp.int32)
    lengths = jnp.concatenate([split, GROUP - split], axis=1)
    live_len = jax.random.randint(jax.random.fold_in(key, 202), (groups, 2), lengths // 4, lengths + 1, dtype=jnp.int32)
    offset = slot - split * series
    limit = jnp.where(series == 1, live_len[:, 1:2], live_len[:, 0:1])
    live = (offset < limit).astype(jnp.int32)
    return (series.reshape(TOKENS), live.reshape(TOKENS))


def draw_series_ids(key, part):
    return series_layout(key)[0]


def draw_live_mask(key, part):
    return series_layout(key)[1]


def block_levels(key, dims, cuts, low, top_value):
    level, own = 1.0, jax.random.fold_in(key, 6)
    for dim, parts in cuts:
        steps = jnp.exp(jax.random.uniform(jax.random.fold_in(own, dim), (parts,), jnp.float32, low / len(cuts), top_value / len(cuts)))
        level = level * jnp.repeat(steps, dims[dim] // parts).reshape([-1 if axis == dim else 1 for axis in range(len(dims))])
    return level


def noise(own_key, shape, scale, most, cuts=(), kind=jnp.bfloat16):
    drawn = jax.random.normal(own_key, shape, jnp.float32) * scale
    if len(cuts) > 0:
        drawn = block_levels(own_key, shape, cuts, -0.22, 0.18) * drawn
    return jnp.clip(drawn, min=-most, max=most).astype(kind)


def setup_inputs(seed: int = 0) -> dict:
    splits = jax.random.split(jax.random.key(seed), 16)
    tokens = noise(splits[0], (TOKENS, D), 1.0, 6.0, ((0, 32),))
    teacher = noise(splits[1], (TOKENS, D), 1.0, 6.0, ((0, 32),))
    series_ids = draw_series_ids(jax.random.fold_in(splits[15], 71), 0)
    live_mask = draw_live_mask(jax.random.fold_in(splits[15], 71), 0)
    gain_one = jnp.clip(1.0 + 0.15 * jax.random.normal(splits[4], (D,), jnp.float32), 0.25, 1.75).astype(jnp.bfloat16)
    query_scale = jnp.clip(jnp.exp(jax.random.uniform(splits[5], (HEAD_DIM,), jnp.float32, math.log(0.69921875), math.log(2.1875))), 0.69921875, 2.1875).astype(jnp.bfloat16)
    query_weight = noise(splits[6], (D, D), D ** -0.5, 0.15625, ((0, 32),))
    key_weight = noise(splits[7], (D, D), D ** -0.5, 0.15625, ((0, 32),))
    value_weight = noise(splits[8], (D, D), D ** -0.5, 0.15625, ((0, 32),))
    attn_out_weight = noise(splits[9], (D, D), (D // 16) ** -0.5, 0.625, ((0, 32),))
    gain_two = jnp.clip(1.0 + 0.15 * jax.random.normal(splits[10], (D,), jnp.float32), 0.25, 1.75).astype(jnp.bfloat16)
    hidden_weight = noise(splits[11], (D, FF), D ** -0.5, 0.15625, ((0, 32),))
    hidden_bias = noise(splits[12], (FF,), 0.3, 1.5, ((0, 32),))
    output_weight = noise(splits[13], (FF, D), FF ** -0.5, 0.15625, ((0, 32),))
    output_bias = noise(splits[14], (D,), 0.3, 1.5, ((0, 32),))
    return dict(tokens=tokens, teacher=teacher, series_ids=series_ids, live_mask=live_mask, gain_one=gain_one, query_scale=query_scale, query_weight=query_weight, key_weight=key_weight, value_weight=value_weight, attn_out_weight=attn_out_weight, gain_two=gain_two, hidden_weight=hidden_weight, hidden_bias=hidden_bias, output_weight=output_weight, output_bias=output_bias)


EPSILON = 1e-06

@jax.custom_vjp
def low(v):
    return lax.optimization_barrier(v.astype(jnp.bfloat16)).astype(jnp.float32)

@jax.custom_vjp
def low_back(v):
    return v

def low_keep(v):
    return (low(v), None)

def low_pass(kept, grad):
    return (grad,)

def back_keep(v):
    return (v, None)

def back_low(kept, grad):
    return (low(grad),)
low.defvjp(low_keep, low_pass)
low_back.defvjp(back_keep, back_low)

def matmul(left, right):
    return jnp.dot(left, right, precision=lax.Precision.HIGHEST, preferred_element_type=jnp.float32)

def rms_normed(inputs, gain):
    return inputs * lax.rsqrt(lax.optimization_barrier(jnp.mean(inputs * inputs, axis=-1, keepdims=True)) + EPSILON) * gain

def group_attention(packed):
    queries, key_rows, value_rows, series, live_slots = packed
    block_rows = min(512, GROUP)
    key_heads = key_rows.reshape(GROUP, HEADS, HEAD_DIM)
    value_heads = value_rows.reshape(GROUP, HEADS, HEAD_DIM)
    key_slots = jnp.arange(GROUP).astype(jnp.int32)

    def one_block(first_slot):
        query_heads = lax.dynamic_slice_in_dim(queries, first_slot, block_rows).reshape(block_rows, HEADS, HEAD_DIM)
        query_series = lax.dynamic_slice_in_dim(series, first_slot, block_rows)
        query_slots = first_slot + jnp.arange(block_rows).astype(jnp.int32)
        scores = low_back(jnp.einsum('qhd,khd->hqk', query_heads, key_heads, precision=lax.Precision.HIGHEST))
        allowed = (query_series[:, None] == series[None, :]) & (key_slots[None, :] <= query_slots[:, None]) & ((live_slots[None, :] > 0) | (key_slots[None, :] == query_slots[:, None]))
        scores = jnp.where(allowed[None], scores, -1e+30)
        row_peak = lax.optimization_barrier(jnp.max(scores, axis=-1, keepdims=True))
        weights = jnp.exp(scores - row_peak)
        probs_low = low(weights / lax.optimization_barrier(jnp.sum(weights, axis=-1, keepdims=True)))
        mixed = jnp.einsum('hqk,khd->qhd', probs_low, value_heads, precision=lax.Precision.HIGHEST)
        return mixed.reshape(block_rows, HEADS * HEAD_DIM)
    firsts = (jnp.arange(GROUP // block_rows) * block_rows).astype(jnp.int32)
    return lax.map(jax.checkpoint(one_block), firsts).reshape(GROUP, HEADS * HEAD_DIM)

def reference(tokens, teacher, series_ids, live_mask, gain_one, query_scale, query_weight, key_weight, value_weight, attn_out_weight, gain_two, hidden_weight, hidden_bias, output_weight, output_bias):
    floats = [item.astype(jnp.float32) for item in (tokens, gain_one, query_scale, query_weight, key_weight, value_weight, attn_out_weight, gain_two, hidden_weight, hidden_bias, output_weight, output_bias)]
    target = teacher.astype(jnp.float32)
    groups = TOKENS // GROUP

    def forward(inputs, gain_a, scale_q, weight_q, weight_k, weight_v, weight_o, gain_b, weight_up, bias_up, weight_down, bias_down):
        normed_one = low(rms_normed(inputs, gain_a))
        query_linear = low_back(matmul(normed_one, weight_q))
        scaled = low(query_linear * jnp.tile(scale_q, HEADS) * (1.0 / math.sqrt(HEAD_DIM)))
        key_rows = low(low_back(matmul(normed_one, weight_k)))
        value_rows = low(low_back(matmul(normed_one, weight_v)))
        mixed = lax.map(jax.checkpoint(group_attention), (scaled.reshape(groups, GROUP, D), key_rows.reshape(groups, GROUP, D), value_rows.reshape(groups, GROUP, D), series_ids.reshape(groups, GROUP), live_mask.reshape(groups, GROUP))).reshape(TOKENS, D)
        mixed = low(low_back(mixed))
        after_attn = inputs + low_back(matmul(mixed, weight_o))
        normed_two = low(rms_normed(after_attn, gain_b))
        pre_act = low_back(matmul(normed_two, weight_up) + bias_up)
        activated = low(jax.nn.silu(pre_act))
        result = after_attn + low_back(matmul(activated, weight_down) + bias_down)
        live_rows = live_mask.astype(jnp.float32)[:, None]
        live_count = jnp.sum(live_rows)
        missed = result - target
        loss_value = jnp.sum(live_rows * missed * missed) / (live_count * D)
        return (loss_value, result)
    loss_value, pullback, result = jax.vjp(forward, *floats, has_aux=True)
    grads = pullback(jnp.asarray(TOKENS * D, dtype=jnp.float32))
    return (result.astype(jnp.bfloat16), loss_value, grads[0], grads[1], grads[2], grads[3], grads[4], grads[5], grads[6], grads[7], grads[8], grads[9], grads[10], grads[11])
```

```python
import functools
import math

import jax
import jax.numpy as jnp
from jax import lax
from jax.experimental import pallas as pl
from jax.experimental.pallas import tpu as pltpu
from jax.sharding import PartitionSpec as P

EPSILON = 1e-06
BOTH = ("dp", "fsdp")
F32 = jnp.float32
BF16 = jnp.bfloat16
LANES = 128
VMEM_LIMIT = 60 * 1024 * 1024


def dot(left, right):
    return jnp.dot(left, right, preferred_element_type=F32)


def dot_nt(left, right):
    return lax.dot_general(left, right, (((1,), (1,)), ((), ())), preferred_element_type=F32)


def dot_tn(left, right):
    return lax.dot_general(left, right, (((0,), (0,)), ((), ())), preferred_element_type=F32)


def front_kernel(
    head, heads, scal, t0, t1, t2, t3, gain, weight, scale_row,
    hidden, qkv, peak, o0, o1, o2, o3, bias, mixed,
):
    rows = t0.shape[0]
    slots = hidden.shape[0]
    width = heads * head
    inv_root = 1.0 / math.sqrt(head)
    qkv[...] = jnp.zeros_like(qkv)
    for rel, piece in enumerate((t0, t1, t2, t3)):
        first = pl.multiple_of(scal[4 + rel] * rows, rows)
        x = piece[...].astype(F32)
        factor = lax.rsqrt(jnp.mean(x * x, axis=1, keepdims=True) + EPSILON)
        low = (x * factor * gain[...].astype(F32)).astype(BF16)
        hidden[pl.ds(first, rows), :] = low
        lin = dot(low, weight[...])
        q = lin[:, :width] * scale_row[...] * inv_root
        parts = (q, lin[:, width : 2 * width], lin[:, 2 * width :])
        for kind, part in enumerate(parts):
            for h in range(heads):
                qkv[kind * heads + h, pl.ds(first, rows), :head] = part[
                    :, h * head : (h + 1) * head
                ].astype(BF16)
    split, live_a, live_b = scal[0], scal[1], scal[2]
    blocks = slots // rows
    for b in range(blocks):
        i = lax.broadcasted_iota(jnp.int32, (rows, slots), 0) + b * rows
        j = lax.broadcasted_iota(jnp.int32, (rows, slots), 1)
        start = jnp.where(i >= split, split, 0)
        stop = jnp.where(i >= split, split + live_b, live_a)
        allowed = ((j >= start) & (j < stop) & (j <= i)) | (j == i)
        bias[b * rows : (b + 1) * rows, :] = jnp.where(allowed, 0.0, -1e30)

    def one_head(h, carry):
        for b in range(blocks):
            seen = (b + 1) * rows
            block = slice(b * rows, seen)
            s = dot_nt(qkv[h, block, :], qkv[heads + h, :seen, :]) + bias[block, :seen]
            top = jnp.max(s, axis=1, keepdims=True)
            e = jnp.exp(s - top)
            total = jnp.sum(e, axis=1, keepdims=True)
            p = (e * (1.0 / total)).astype(BF16)
            peak[h, block, :] = top + jnp.log(total)
            mixed[h, block, :] = dot(p, qkv[2 * heads + h, :seen, :]).astype(BF16)
        return carry

    lax.fori_loop(0, heads, one_head, 0)
    for rel, out in enumerate((o0, o1, o2, o3)):
        first = pl.multiple_of(scal[4 + rel] * rows, rows)
        out[...] = jnp.concatenate(
            [mixed[h, pl.ds(first, rows), :][:, :head] for h in range(heads)], axis=1
        )


def mid_kernel(
    scal, step, tokens, teacher, o0, o1, o2, o3, wo, wh, wu, vec,
    block_out, gx1, g0, g1, g2, g3, grads, small,
):
    rows, width = tokens.shape
    part = o0.shape[1]
    tile = 256
    slot = lax.broadcasted_iota(jnp.int32, (rows, 1), 0) + scal[4] * rows
    stop = jnp.where(slot >= scal[0], scal[0] + scal[2], scal[1])
    live = (slot < stop).astype(F32)
    pieces = (o0, o1, o2, o3)
    firsts = [pl.multiple_of(scal[4 + rel] * part, part) for rel in range(4)]
    x1 = tokens[...].astype(F32)
    for rel in range(4):
        x1 = x1 + dot(pieces[rel][...], wo[pl.ds(firsts[rel], part), :])
    factor = lax.rsqrt(jnp.mean(x1 * x1, axis=1, keepdims=True) + EPSILON)
    n2 = x1 * factor
    gain = vec[0:1, :]
    h2 = (n2 * gain).astype(BF16)
    z = dot(h2, wh[...]) + vec[1:2, :]
    sig = 1.0 / (1.0 + jnp.exp(-z))
    act = (z * sig).astype(BF16)
    y = x1 + (dot(act, wu[...]) + vec[2:3, :])
    block_out[...] = y.astype(BF16)
    missed = y - teacher[...].astype(F32)
    gy = missed * live * step[0]
    gyb = gy.astype(BF16)
    small[3:4, :] = jnp.sum(live * missed * missed, axis=0, keepdims=True)
    small[2:3, :] = jnp.sum(gyb.astype(F32), axis=0, keepdims=True)
    for i in range(width // tile):
        cols = slice(i * tile, (i + 1) * tile)
        grads[2, cols, :] = dot_tn(act[:, cols], gyb).astype(BF16)
    gz = (dot_nt(gyb, wu[...]) * sig * (1.0 + z * (1.0 - sig))).astype(BF16)
    small[1:2, :] = jnp.sum(gz.astype(F32), axis=0, keepdims=True)
    for i in range(width // tile):
        cols = slice(i * tile, (i + 1) * tile)
        grads[1, cols, :] = dot_tn(h2[:, cols], gz).astype(BF16)
    gh2 = dot_nt(gz, wh[...])
    small[0:1, :] = jnp.sum(gh2 * n2, axis=0, keepdims=True)
    small[4:8, :] = jnp.zeros((4, width), F32)
    gn2 = gh2 * gain
    back = gy + factor * (gn2 - n2 * jnp.mean(gn2 * n2, axis=1, keepdims=True))
    gx1[...] = back
    low = back.astype(BF16)
    for rel, out in enumerate((g0, g1, g2, g3)):
        grads[0, pl.ds(firsts[rel], part), :] = dot_tn(pieces[rel][...], low).astype(BF16)
        out[...] = dot_nt(low, wo[pl.ds(firsts[rel], part), :]).astype(BF16)


def back_kernel(
    head, heads, scal, hidden, qkv, peak, g0, g1, g2, g3, weight, gain, scale_pad,
    grads, own, other, cross, small, bias, upstream, gpad, gk, gv, packed,
):
    rows = g0.shape[0]
    slots = hidden.shape[0]
    width = hidden.shape[1]
    blocks = slots // rows
    inv_root = 1.0 / math.sqrt(head)
    upstream[...] = jnp.zeros_like(upstream)
    for rel, piece in enumerate((g0, g1, g2, g3)):
        first = pl.multiple_of(scal[4 + rel] * rows, rows)
        for h in range(heads):
            upstream[h, pl.ds(first, rows), :head] = piece[:, h * head : (h + 1) * head]
    split, live_a, live_b = scal[0], scal[1], scal[2]
    for b in range(blocks):
        i = lax.broadcasted_iota(jnp.int32, (rows, slots), 0) + b * rows
        j = lax.broadcasted_iota(jnp.int32, (rows, slots), 1)
        start = jnp.where(i >= split, split, 0)
        stop = jnp.where(i >= split, split + live_b, live_a)
        allowed = ((j >= start) & (j < stop) & (j <= i)) | (j == i)
        bias[b * rows : (b + 1) * rows, :] = jnp.where(allowed, 0.0, -1e30)

    def one_head(h, scale_sum):
        gk[...] = jnp.zeros_like(gk)
        gv[...] = jnp.zeros_like(gv)
        for b in range(blocks):
            seen = (b + 1) * rows
            block = slice(b * rows, seen)
            q = qkv[h, block, :]
            k = qkv[heads + h, :seen, :]
            up = upstream[h, block, :]
            s = dot_nt(q, k) + bias[block, :seen]
            p32 = jnp.exp(s - peak[h, block, :])
            gp = dot_nt(up, qkv[2 * heads + h, :seen, :])
            c = jnp.sum(p32 * gp, axis=1, keepdims=True)
            gs = (p32 * (gp - c)).astype(BF16)
            p = p32.astype(BF16)
            gq = dot(gs, k)
            scale_sum = scale_sum + jnp.sum(gq * q.astype(F32), axis=0, keepdims=True)
            gpad[h, block, :] = (gq * scale_pad[...] * inv_root).astype(BF16)
            gk[:seen, :] += dot_tn(gs, q)
            gv[:seen, :] += dot_tn(p, up)
        gpad[heads + h] = gk[...].astype(BF16)
        gpad[2 * heads + h] = gv[...].astype(BF16)
        return scale_sum

    scale_sum = lax.fori_loop(0, heads, one_head, jnp.zeros((1, LANES), F32))
    small[...] = jnp.zeros_like(small)
    small[1:2, :LANES] = scale_sum
    for b in range(blocks):
        block = slice(b * rows, (b + 1) * rows)
        packed[block, :] = jnp.concatenate(
            [gpad[n, block, :][:, :head] for n in range(3 * heads)], axis=1
        )
    tile = 256
    for i in range(width // tile):
        cols = slice(i * tile, (i + 1) * tile)
        grads[cols, :] = dot_tn(hidden[:, cols], packed[...]).astype(BF16)
    gain_sum = jnp.zeros((1, width), F32)
    for rel in range(4):
        first = pl.multiple_of(scal[4 + rel] * rows, rows)
        part = dot_nt(packed[pl.ds(first, rows), :], weight[...])
        gain_sum = gain_sum + jnp.sum(
            part * hidden[pl.ds(first, rows), :].astype(F32), axis=0, keepdims=True
        )
        if rel == 0:
            own[...] = part
        elif rel == 2:
            other[...] = part
        else:
            cross[rel // 2] = part.astype(BF16)
    small[0:1, :] = gain_sum / gain[...].astype(F32)


def call(kernel, name, outs, scratch, args, smem, flops):
    full = pl.BlockSpec(memory_space=pltpu.VMEM)
    scalar = pl.BlockSpec(memory_space=pltpu.SMEM)
    moved = sum(a.size * a.dtype.itemsize for a in args)
    moved += sum(math.prod(o.shape) * o.dtype.itemsize for o in outs)
    return pl.pallas_call(
        kernel,
        out_shape=outs,
        in_specs=[scalar] * smem + [full] * (len(args) - smem),
        out_specs=[full] * len(outs),
        scratch_shapes=scratch,
        compiler_params=pltpu.CompilerParams(vmem_limit_bytes=VMEM_LIMIT),
        cost_estimate=pl.CostEstimate(flops=flops, bytes_accessed=moved, transcendentals=0),
        name=name,
    )(*args)


def sds(shape, dtype):
    return jax.ShapeDtypeStruct(shape, dtype)


def moved(x, dp, fsdp, to):
    pairs = [(d * fsdp + f, to(d, f)[0] * fsdp + to(d, f)[1]) for d in range(dp) for f in range(fsdp)]
    return lax.ppermute(x, BOTH, pairs)


def at(x, index, axis):
    return lax.dynamic_index_in_dim(x, index, axis, keepdims=False)


def local(
    dp,
    fsdp,
    tokens,
    teacher,
    series_ids,
    live_mask,
    gain_one,
    query_scale,
    query_weight,
    key_weight,
    value_weight,
    attn_out_weight,
    gain_two,
    hidden_weight,
    hidden_bias,
    output_weight,
    output_bias,
):
    rows, width = tokens.shape
    head = query_scale.shape[0]
    owners = dp * fsdp
    share = query_weight.shape[0]
    part = width // fsdp
    heads = part // head
    slots = rows * fsdp
    total_slots = rows * owners
    d = lax.axis_index("dp")
    f = lax.axis_index("fsdp")
    fast = dp == 8
    send = functools.partial(moved, dp=dp, fsdp=fsdp)

    def swap(x, r):
        return send(x, to=lambda a, b: (a, b ^ r))

    def swap_x(x):
        return send(x, to=lambda a, b: (a ^ 1, b))

    def shift_z(x, s):
        return send(x, to=lambda a, b: ((a // 2 + s) % 4 * 2 + a % 2, b))

    t_core = swap(tokens, 1)
    t_y = swap(tokens, 2)
    t_yc = swap(t_y, 1)

    first_series = (series_ids == 0).astype(F32)
    live = live_mask.astype(F32)
    counts = jnp.stack(
        [jnp.sum(first_series), jnp.sum(first_series * live), jnp.sum((1.0 - first_series) * live)]
    )
    vectors = jnp.concatenate([gain_one, gain_two, hidden_bias, output_bias])
    ext = jnp.concatenate([vectors, counts.astype(BF16)])
    ext = jnp.pad(ext, (0, part * 3 // fsdp - ext.shape[0]))[None, :]

    packs = jnp.concatenate(
        [w.reshape(share, fsdp, part) for w in (query_weight, key_weight, value_weight)], axis=2
    ).transpose(1, 0, 2)
    if fast:
        extra = jnp.pad(ext, ((0, 7), (0, 3 * part - ext.shape[1])))
        packs = jnp.concatenate([packs, jnp.broadcast_to(extra[None], (fsdp,) + extra.shape)], axis=1)
        got = [at(packs, f, 0)] + [swap(at(packs, f ^ r, 0), r) for r in range(1, 4)]
        block = jnp.zeros((fsdp,) + got[0].shape, BF16)
        for r in range(4):
            block = lax.dynamic_update_index_in_dim(block, got[r], f ^ r, 0)
        line = block[:, share, : ext.shape[1]].reshape(1, 3 * part)
        line = jnp.pad(line, ((0, 7), (0, 0)))
        block = jnp.concatenate([block[:, :share].reshape(fsdp * share, 3 * part), line], axis=0)
        z_parts = [block] + [shift_z(block, s) for s in range(1, 4)]
        x_parts = [swap_x(b) for b in z_parts]
        z, x = d // 2, d % 2
        gathered = jnp.zeros((dp,) + block.shape, BF16)
        for s in range(4):
            zi = (z - s) % 4
            gathered = lax.dynamic_update_index_in_dim(gathered, z_parts[s], zi * 2 + x, 0)
            gathered = lax.dynamic_update_index_in_dim(gathered, x_parts[s], zi * 2 + (1 - x), 0)
        qkv_weight = gathered[:, : fsdp * share].reshape(width, 3 * part)
        every = gathered[:, fsdp * share].reshape(owners, ext.shape[1])
    else:
        got = lax.all_to_all(packs, "fsdp", 0, 0, tiled=True)
        qkv_weight = lax.all_gather(got.reshape(fsdp * share, 3 * part), "dp", axis=0, tiled=True)
        every = lax.all_gather(ext, BOTH, axis=0, tiled=True)
    full_gain_one, full_gain_two, full_hidden_bias, full_output_bias = [
        every[:, n * share : (n + 1) * share].reshape(1, width) for n in range(4)
    ]
    numbers = every[:, 4 * share : 4 * share + 3].astype(F32)
    live_count = jnp.sum(numbers[:, 1:])
    mine = jnp.sum(lax.dynamic_slice_in_dim(numbers, d * fsdp, fsdp, 0), axis=0).astype(jnp.int32)
    scal = jnp.concatenate(
        [mine, jnp.zeros((1,), jnp.int32), (f ^ jnp.arange(4, dtype=jnp.int32)).astype(jnp.int32)]
    )

    rest = jnp.concatenate([attn_out_weight, hidden_weight, output_weight], axis=0)
    rest = lax.all_gather(rest, BOTH, axis=0, tiled=True).reshape(owners, 3, share, width)
    wo, wh, wu = [rest[:, n].reshape(width, width) for n in range(3)]

    scale = query_scale.astype(F32)
    scale_row = jnp.tile(scale, heads)[None, :]
    scale_pad = jnp.pad(scale, (0, LANES - head))[None, :]
    front_flops = 2 * slots * width * 3 * part + 4 * heads * slots * slots * LANES
    hidden, qkv, peak, o0, o1, o2, o3 = call(
        functools.partial(front_kernel, head, heads),
        "front",
        [
            sds((slots, width), BF16),
            sds((3 * heads, slots, LANES), BF16),
            sds((heads, slots, 1), F32),
        ]
        + [sds((rows, part), BF16)] * 4,
        [pltpu.VMEM((slots, slots), F32), pltpu.VMEM((heads, slots, LANES), BF16)],
        (scal, tokens, t_core, t_y, t_yc, full_gain_one, qkv_weight, scale_row),
        1,
        front_flops,
    )
    o_parts = [o0] + [swap(o, r) for r, o in ((1, o1), (2, o2), (3, o3))]
    step = (2.0 * total_slots / live_count).reshape(1)
    vec = jnp.concatenate([full_gain_two, full_hidden_bias, full_output_bias], axis=0).astype(F32)
    vec = jnp.pad(vec, ((0, 5), (0, 0)))
    block_out, gx1, g0, g1, g2, g3, mlp_grads, mid_small = call(
        mid_kernel,
        "mid",
        [sds((rows, width), BF16), sds((rows, width), F32)]
        + [sds((rows, part), BF16)] * 4
        + [sds((3, width, width), BF16), sds((8, width), F32)],
        [],
        (scal, step, tokens, teacher, *o_parts, wo, wh, wu, vec),
        2,
        18 * rows * width * width,
    )
    g_parts = [g0] + [swap(g, r) for r, g in ((1, g1), (2, g2), (3, g3))]

    if fast:
        y, c = f // 2, f % 2
        sums = mlp_grads.reshape(3, 4, 2, 2, 2, share, width)
        got = swap(at(sums, 1 - c, 4), 1)
        sums = at(sums, c, 4).astype(F32) + got.astype(F32)

        def corner(xr, yr):
            return at(at(sums, x ^ xr, 2), y ^ yr, 2)

        here = corner(0, 0)
        for xr, yr in ((1, 0), (0, 1), (1, 1)):
            away = corner(xr, yr).astype(BF16)
            here = here + send(away, to=lambda a, b: (a ^ xr, b ^ (2 * yr))).astype(F32)
        mlp_share = at(here, z, 1)
        for s in range(1, 4):
            mlp_share = mlp_share + shift_z(at(here, (z + s) % 4, 1).astype(BF16), s).astype(F32)
    else:
        sums = mlp_grads.reshape(3, owners, share, width).transpose(1, 0, 2, 3)
        sums = sums.reshape(owners, 3 * share * width)
        mlp_share = lax.psum_scatter(sums, BOTH, scatter_dimension=0, tiled=True)
        mlp_share = mlp_share.reshape(3, share, width).astype(F32)

    back_flops = 4 * slots * width * 3 * part + 10 * heads * slots * slots * LANES
    qkv_grads, own, other, cross, back_small = call(
        functools.partial(back_kernel, head, heads),
        "back",
        [
            sds((width, 3 * part), BF16),
            sds((rows, width), F32),
            sds((rows, width), F32),
            sds((2, rows, width), BF16),
            sds((8, width), F32),
        ],
        [
            pltpu.VMEM((slots, slots), F32),
            pltpu.VMEM((heads, slots, LANES), BF16),
            pltpu.VMEM((3 * heads, slots, LANES), BF16),
            pltpu.VMEM((slots, LANES), F32),
            pltpu.VMEM((slots, LANES), F32),
            pltpu.VMEM((slots, 3 * part), BF16),
        ],
        (scal, hidden, qkv, peak, *g_parts, qkv_weight, full_gain_one, scale_pad),
        1,
        back_flops,
    )
    cross = swap(cross, 1)
    other = swap((other + cross[1].astype(F32)).astype(BF16), 2)
    grad_normed = own + cross[0].astype(F32) + other.astype(F32)
    inputs = tokens.astype(F32)
    factor = lax.rsqrt(jnp.mean(inputs * inputs, axis=1, keepdims=True) + EPSILON)
    normed = inputs * factor
    scaled = grad_normed * full_gain_one.astype(F32)
    grad_tokens = gx1 + factor * (scaled - normed * jnp.mean(scaled * normed, axis=1, keepdims=True))

    if fast:
        sums = qkv_grads.reshape(4, 2, fsdp * share, 3 * part)
        got = swap_x(at(sums, 1 - x, 1))
        sums = at(sums, x, 1).astype(F32) + got.astype(F32)
        here = at(sums, z, 0)
        for s in range(1, 4):
            here = here + shift_z(at(sums, (z + s) % 4, 0).astype(BF16), s).astype(F32)
        here = here.astype(BF16).reshape(fsdp, share, 3 * part)
        block = jnp.zeros_like(here)
        block = lax.dynamic_update_index_in_dim(block, at(here, f, 0), f, 0)
        for r in range(1, 4):
            block = lax.dynamic_update_index_in_dim(block, swap(at(here, f ^ r, 0), r), f ^ r, 0)
    else:
        here = lax.psum_scatter(qkv_grads, "dp", scatter_dimension=0, tiled=True)
        block = lax.all_to_all(here.reshape(fsdp, share, 3 * part), "fsdp", 0, 0, tiled=True)
    block = block.reshape(fsdp, share, 3, part).transpose(2, 1, 0, 3).reshape(3, share, width)
    block = block.astype(F32)

    flat = jnp.concatenate(
        [
            back_small[0],
            mid_small[0],
            mid_small[1],
            mid_small[2],
            back_small[1, :head] / scale,
            jnp.sum(mid_small[3])[None],
        ]
    )
    flat = lax.psum(jnp.pad(flat, (0, -flat.shape[0] % LANES)), BOTH)
    lines = flat[: 4 * width].reshape(4, owners, share)
    lines = at(lines, d * fsdp + f, 1)
    scale_total = flat[4 * width : 4 * width + head]
    loss_value = flat[4 * width + head] / (live_count * width)
    return (
        block_out,
        loss_value,
        grad_tokens,
        lines[0],
        scale_total,
        block[0],
        block[1],
        block[2],
        mlp_share[0],
        lines[1],
        mlp_share[1],
        lines[2],
        mlp_share[2],
        lines[3],
    )


def solution(mesh):
    dp, fsdp = mesh.shape["dp"], mesh.shape["fsdp"]
    row, line = P(BOTH, None), P(BOTH)
    return jax.shard_map(
        functools.partial(local, dp, fsdp),
        mesh=mesh,
        in_specs=(row, row, line, line, line, P(), row, row, row, row, line, row, line, row, line),
        out_specs=(row, P(), row, line, P(), row, row, row, row, line, row, line, row, line),
        check_vma=False,
    )
```
